32 devices in a mesh: req: 8 (over z, x), head: 4 (over y, core).
Axes of the slice: x: 2, y: 2, z: 4, core: 2. Of those that a mesh axis runs over, the one named last changes fastest.
Arguments:
- residual_in: bfloat16 [1024, 1536], P(('req', 'head')), may hold values from -3 to 3
- attn_gain: bfloat16 [1536], replicated, may hold values from 0.099609375 to 1.8984375
- w_qkv: bfloat16 [1536, 8, 320], P(None, 'head'), may hold values from -0.15625 to 0.15625
- w_out: bfloat16 [1536, 1536], P('head'), may hold values from -0.41992188 to 0.41992188
- kv_cache: bfloat16 [1024, 8, 192, 128], P('req', 'head'), as said below
- lengths: int32 [1024], P('req'), may hold values from 1 to 192, as said below
- moe_gain: bfloat16 [1536], replicated, may hold values from 0.099609375 to 1.8984375
- w_router: bfloat16 [1536, 24], replicated
- routes: int32 [1024, 8], P(('req', 'head')), may hold values from 0 to 23, all different within a row; in each aligned block of 32 rows (0 to 31, 32 to 63, ...) at most 12 rows name the same one
- w_in: bfloat16 [24, 1536, 1024], P('req'), may hold values from -0.15625 to 0.15625
- w_down: bfloat16 [24, 512, 1536], P('req'), may hold values from -0.5 to 0.5
Outputs:
- layer_out: bfloat16 [1024, 1536], P(('req', 'head'))
- new_kv: bfloat16 [1024, 8, 128], P('req', 'head')
The draws below stay inside these ranges and needn't reach their ends.
Inputs may be any that keep to these rules, and one draw needn't show every extreme that they name: `kv_cache`: each position holds its key in the first 64 entries and its value in the last 64. `lengths`: some request has exactly 192 cached positions. `routes`: each row names 8 different experts. Among the 32 rows of one device no expert is named more than 12 times, a bound that some block reaches.
All inputs are finite; a program needn't handle non-finite values.
Results may differ from the reference program's by a relative error of at most 0.017.
Values may be sent and summed in bfloat16 or wider, within the bound.
A program may use at most 128 MiB of HBM per device.

```python
import math
import jax
import jax.numpy as jnp
import numpy as np
from jax import lax

D = 1536
HEADS = 24
KV = 8
HD = 64
F = 512
TOPK = 8
B_DEV = 128
LMAX = 192
EXPERTS = 24
REQUESTS = 1024
T_DEV = 32
CAP = 12


def draw_lengths(key, part):
    first, second, third = jax.random.split(key, 3)
    groups = REQUESTS // B_DEV
    level = jax.random.randint(first, (groups,), 0, 4)
    table = jnp.array([LMAX, LMAX // 2, LMAX // 4, LMAX // 8], jnp.int32)
    ceiling = jnp.repeat(table[level], B_DEV)
    raw = jax.random.randint(second, (REQUESTS,), 0, LMAX)
    counts = 1 + raw % ceiling
    chosen = jax.random.randint(third, (), 0, REQUESTS)
    return jnp.where(jnp.arange(REQUESTS) == chosen, LMAX, counts).astype(jnp.int32)


def draw_kv_cache(key, part):
    first = jax.random.fold_in(key, 0)
    shape = (REQUESTS, KV, LMAX, 2 * HD)
    base = jnp.clip(jax.random.normal(first, shape, jnp.float32), -6.0, 6.0)
    return base.astype(jnp.bfloat16)


def draw_w_router(key, part):
    first, second = jax.random.split(key, 2)
    base = jnp.clip(jax.random.normal(first, (D, EXPERTS), jnp.float32), -6.0, 6.0) * D ** (-0.5)
    scale = 0.4 * jnp.exp(jax.random.uniform(second, (1, EXPERTS), minval=0.0, maxval=1.1))
    return (base * scale).astype(jnp.bfloat16)


def block_scale(own_key, shape, cuts, low, top_value):
    factor_of = 1.0
    for axis_at, blocks in cuts:
        steps = jax.random.uniform(jax.random.fold_in(jax.random.fold_in(own_key, 6), axis_at), (blocks,), jnp.float32, low / len(cuts), top_value / len(cuts))
        factor_of = factor_of * jnp.repeat(jnp.exp(steps), shape[axis_at] // blocks).reshape((-1,) + (1,) * (len(shape) - 1 - axis_at))
    return factor_of


def deal_out(rng, own, number, rows, amount, top, reach, skew):
    ranking = jax.random.permutation(rng, amount)
    packed, usual = load_shares(amount, rows * top, reach, skew, True), load_shares(amount, rows * top, reach, skew, False)
    places = jnp.arange(amount)

    def named(tallies, rotation):
        used = int((tallies > 0).sum())
        fixed = max(1, used // 4)
        shifted = fixed + (places - fixed + rotation * (used - fixed)) % max(1, amount - fixed)
        return jnp.zeros((amount,), jnp.int32).at[ranking[jnp.where(places < fixed, places, shifted)]].set(jnp.asarray(tallies, jnp.int32))

    tallies = jnp.where(number % 4 == 0, named(packed, number // 4), named(usual, number - number // 4 - 1))
    mixed = jax.random.permutation(jax.random.fold_in(own, 3), amount)
    donor, receiver = mixed[0:amount // 2 * 2:2], mixed[1:amount // 2 * 2:2]
    slack = jnp.minimum(tallies[donor] - 1, reach - tallies[receiver]) // 2
    slack = jnp.where((donor == ranking[0]) | (receiver == ranking[0]) | (tallies[receiver] == 0), 0, jnp.maximum(slack, 0))
    shifted = jax.random.randint(jax.random.fold_in(own, 4), (amount // 2,), 0, 1 << 20) % (slack + 1)
    tallies = tallies.at[donor].add(-shifted).at[receiver].add(shifted)
    labels = jnp.searchsorted(jnp.cumsum(tallies), jnp.arange(rows * top), side="right").astype(jnp.int32)
    listing = labels.reshape(top, rows).T
    listing = listing[jax.random.permutation(jax.random.fold_in(own, 1), rows)]
    rotation = jax.random.randint(jax.random.fold_in(own, 2), (rows, 1), 0, top)
    return jnp.take_along_axis(listing, (jnp.arange(top)[None, :] + rotation) % top, axis=1)


def load_shares(number_of, total, reach, slope, full):
    loads = [(1 << 20) // math.isqrt(standing ** slope) + 1 for standing in range(1, number_of + 1)]
    largest = reach if full else min(reach, max(-(-total // number_of), total * loads[0] // sum(loads)))
    least = 1 if total - largest >= number_of - 1 else 0
    given, rest = [largest] + [least] * (number_of - 1), total - largest - least * (number_of - 1)
    while rest > 0:
        movable = [i for i in range(1, number_of) if given[i] < largest] or [i for i in range(1, number_of) if given[i] < reach]
        mass, remaining = sum([loads[i] for i in movable]), rest
        for i in movable:
            extra = min(reach - given[i], max(1, remaining * loads[i] // mass), rest)
            given[i] = given[i] + extra
            rest = rest - extra
    return np.array(given)


def centred(own_key, extent, spread, most, cuts=(), kind=jnp.bfloat16):
    level = block_scale(own_key, extent, cuts, -0.22, 0.18) if cuts else 1.0
    result = jax.random.normal(own_key, extent, jnp.float32) * spread * level
    return jnp.minimum(jnp.maximum(result, -most), most).astype(kind)


def setup_inputs(seed: int = 0) -> dict:
    key_list = jax.random.split(jax.random.key(seed), 12)
    residual_in = centred(key_list[0], (REQUESTS, D), 0.5, 3.0, ((0, 32),))
    attn_gain = jnp.clip(1.0 + 0.18 * jax.random.normal(key_list[1], (D,), jnp.float32), 0.099609375, 1.8984375).astype(jnp.bfloat16)
    w_qkv = centred(key_list[2], (D, KV, (HEADS // KV + 2) * HD), D ** -0.5, 0.15625, ((1, 4),))
    w_out = centred(key_list[3], (HEADS * HD, D), 0.07, 0.41992188, ((0, 4),))
    kv_cache = draw_kv_cache(jax.random.fold_in(key_list[11], 71), 0)
    lengths = draw_lengths(jax.random.fold_in(key_list[11], 71), 0)
    moe_gain = jnp.clip(1.0 + 0.18 * jax.random.normal(key_list[6], (D,), jnp.float32), 0.099609375, 1.8984375).astype(jnp.bfloat16)
    w_router = draw_w_router(jax.random.fold_in(key_list[11], 71), 0)
    routes_keys = jax.random.split(jax.random.fold_in(key_list[8], 1), REQUESTS // T_DEV)
    routes_turns = jax.random.permutation(jax.random.fold_in(key_list[8], 3), REQUESTS // T_DEV)
    routes = jax.vmap(lambda own, number: deal_out(jax.random.fold_in(key_list[8], 2), own, number, T_DEV, EXPERTS, TOPK, CAP, 2))(routes_keys, routes_turns).reshape((REQUESTS, TOPK))
    w_in = centred(key_list[9], (EXPERTS, D, 2 * F), D ** -0.5, 0.15625, ((0, 8),))
    w_down = centred(key_list[10], (EXPERTS, F, D), (F // 4) ** -0.5, 0.5, ((0, 8),))
    return {"residual_in": residual_in, "attn_gain": attn_gain, "w_qkv": w_qkv, "w_out": w_out, "kv_cache": kv_cache, "lengths": lengths, "moe_gain": moe_gain, "w_router": w_router, "routes": routes, "w_in": w_in, "w_down": w_down}


EPSILON = 1e-06
THETA = 10000.0

def rms_scale(values, gain):
    wide = values.astype(jnp.float32)
    mean_square = lax.optimization_barrier(jnp.mean(wide * wide, axis=-1, keepdims=True))
    return (wide * lax.rsqrt(mean_square + EPSILON) * gain.astype(jnp.float32)).astype(jnp.bfloat16)

def rotate(vectors, lengths):
    half = vectors.shape[-1] // 2
    index = jnp.arange(half).astype(jnp.float32)
    frequency = jnp.power(THETA, -2.0 * index / vectors.shape[-1])
    angle = lengths.astype(jnp.float32)[:, None] * frequency[None, :]
    cosine = jnp.cos(angle)[:, None, None, :]
    sine = jnp.sin(angle)[:, None, None, :]
    first = vectors[..., :half]
    second = vectors[..., half:]
    return jnp.concatenate([first * cosine - second * sine, second * cosine + first * sine], axis=-1)

def project_heads(projected, lengths, group, head_size):
    blocks = projected.reshape(projected.shape[0], -1, group + 2, head_size)
    queries = rotate(blocks[:, :, :group], lengths).astype(jnp.bfloat16)
    new_keys = rotate(blocks[:, :, group:group + 1], lengths).astype(jnp.bfloat16)[:, :, 0]
    new_values = blocks[:, :, group + 1].astype(jnp.bfloat16)
    return (queries, new_keys, new_values)

def attend(items):
    queries, new_keys, new_values, cache, lengths = items
    head_size = queries.shape[-1]
    scale = head_size ** (-0.5)
    keys = cache[..., :head_size].astype(jnp.float32)
    values = cache[..., head_size:].astype(jnp.float32)
    scores = jnp.einsum('rkgd,rkld->rkgl', queries.astype(jnp.float32), keys) * scale
    own = lax.optimization_barrier(jnp.sum(queries.astype(jnp.float32) * new_keys.astype(jnp.float32)[:, :, None, :], axis=-1)) * scale
    positions = jnp.arange(cache.shape[2]).astype(jnp.int32)
    live = (positions[None, :] < lengths[:, None])[:, None, None, :]
    masked = jnp.where(live, scores, -1e+30)
    peak = jnp.maximum(lax.optimization_barrier(jnp.max(masked, axis=-1)), own)
    weights = jnp.where(live, jnp.exp(masked - peak[..., None]), 0.0)
    own_weight = jnp.exp(own - peak)
    total = lax.optimization_barrier(jnp.sum(weights, axis=-1)) + own_weight
    probabilities = weights.astype(jnp.bfloat16)
    own_prob = own_weight.astype(jnp.bfloat16)
    weighted = jnp.einsum('rkgl,rkld->rkgd', probabilities.astype(jnp.float32), values)
    weighted = weighted + own_prob.astype(jnp.float32)[..., None] * new_values.astype(jnp.float32)[:, :, None, :]
    return (weighted / total[..., None]).astype(jnp.bfloat16)

def reference(residual_in, attn_gain, w_qkv, w_out, kv_cache, lengths, moe_gain, w_router, routes, w_in, w_down):
    group = HEADS // KV
    normed = rms_scale(residual_in, attn_gain)
    projected = jnp.dot(normed, w_qkv.reshape(D, KV * (group + 2) * HD), preferred_element_type=jnp.float32)
    queries, new_keys, new_values = project_heads(projected, lengths, group, HD)
    new_kv = jnp.concatenate([new_keys, new_values], axis=-1)
    blocks = REQUESTS // B_DEV
    heads_out = lax.map(attend, (queries.reshape(blocks, B_DEV, KV, group, HD), new_keys.reshape(blocks, B_DEV, KV, HD), new_values.reshape(blocks, B_DEV, KV, HD), kv_cache.reshape(blocks, B_DEV, KV, LMAX, 2 * HD), lengths.reshape(blocks, B_DEV)))
    attn_heads = heads_out.reshape(REQUESTS, HEADS * HD)
    attention = jnp.dot(attn_heads, w_out, preferred_element_type=jnp.float32)
    attended = (residual_in.astype(jnp.float32) + attention).astype(jnp.bfloat16)
    normed_moe = rms_scale(attended, moe_gain)
    logits = jnp.dot(normed_moe, w_router, preferred_element_type=jnp.float32)
    gates = jax.nn.softmax(jnp.take_along_axis(logits, routes, axis=1), axis=-1)
    most_rows = REQUESTS // T_DEV * CAP

    def add_expert(mixed, expert):
        hit = routes == expert
        chosen = jnp.any(hit, axis=1)
        weight = lax.optimization_barrier(jnp.sum(jnp.where(hit, gates, 0.0), axis=1))
        order = jnp.cumsum(chosen.astype(jnp.int32)) - 1
        target = jnp.where(chosen, order, most_rows).astype(jnp.int32)
        picks = jnp.zeros((most_rows,), jnp.int32).at[target].set(jnp.arange(REQUESTS).astype(jnp.int32), mode='drop')
        valid = jnp.zeros((most_rows,), jnp.float32).at[target].set(1.0, mode='drop')
        rows = normed_moe[picks]
        both = jnp.dot(rows, w_in[expert], preferred_element_type=jnp.float32)
        hidden = (jax.nn.silu(both[:, :F]) * both[:, F:]).astype(jnp.bfloat16)
        out_rows = jnp.dot(hidden, w_down[expert], preferred_element_type=jnp.float32).astype(jnp.bfloat16)
        term = out_rows.astype(jnp.float32) * (weight[picks] * valid)[:, None]
        return (mixed.at[picks].add(term), expert)
    mixed = lax.scan(add_expert, jnp.zeros((REQUESTS, D), jnp.float32), jnp.arange(EXPERTS).astype(jnp.int32))[0]
    layer_out = (attended.astype(jnp.float32) + mixed).astype(jnp.bfloat16)
    return (layer_out, new_kv)
```

```python
import functools

import jax
import jax.numpy as jnp
from jax import lax
from jax.experimental import pallas as pl
from jax.experimental.pallas import tpu as pltpu
from jax.sharding import PartitionSpec as P

D = 1536
HEADS = 24
KV = 8
HD = 64
F = 512
GROUP = HEADS // KV
LANES = 128
WIDE = D + LANES

EPSILON = 1e-06
THETA = 10000.0
MESH = pl.DeviceIdType.MESH
BF = jnp.bfloat16
F32 = jnp.float32


def rms_scale(wide, gain):
    mean_square = jnp.mean(wide * wide, axis=-1, keepdims=True)
    return (wide * lax.rsqrt(mean_square + EPSILON) * gain.astype(F32)).astype(BF)


class Axis:
    def __init__(self, name, A, B):
        self.name, self.A, self.B = name, A, B
        me = lax.axis_index(name)
        self.a, self.b = me // B, me % B

    def peers(self):
        A, B = self.A, self.B
        out = [((self.a + d) % A) * B + self.b for d in range(1, A)]
        return out + [self.a * B + (self.b + d) % B for d in range(1, B)]

    def copy(self, src, dst, send, recv, a, b):
        return pltpu.make_async_remote_copy(
            src_ref=src, dst_ref=dst, send_sem=send, recv_sem=recv,
            device_id={self.name: a * self.B + b}, device_id_type=MESH)


def gather_start(ax, buf, send, recv):
    sent = []
    a, b = ax.a, ax.b
    own = buf.at[a, b]
    for d in range(ax.A - 1, 0, -1):
        c = ax.copy(own, own, send.at[d, 0], recv.at[a, b], (a + d) % ax.A, b)
        c.start()
        sent.append(c)
    for d in range(1, ax.B):
        c = ax.copy(own, own, send.at[0, d], recv.at[a, b], a, (b + d) % ax.B)
        c.start()
        sent.append(c)
    return sent


def gather_forward(ax, buf, send, recv, sent):
    a, b = ax.a, ax.b
    for d in range(1, ax.A):
        o = (a + ax.A - d) % ax.A
        block = buf.at[o, b]
        ax.copy(block, block, send.at[0, 0], recv.at[o, b], a, b).wait_recv()
        for e in range(1, ax.B):
            c = ax.copy(block, block, send.at[d, e], recv.at[o, b], a, (b + e) % ax.B)
            c.start()
            sent.append(c)


def gather_column(ax, buf, send, recv, e):
    o = (ax.b + ax.B - e) % ax.B
    for d in range(ax.A):
        a = (ax.a + ax.A - d) % ax.A
        block = buf.at[a, o]
        ax.copy(block, block, send.at[0, 0], recv.at[a, o], ax.a, ax.b).wait_recv()
    return o


def scatter_minor(ax, part, rx, send, recv, e, sent):
    t = (ax.b + e) % ax.B
    for d in range(1, ax.A + 1):
        a = (ax.a + d) % ax.A
        c = ax.copy(part.at[a, t], rx.at[e - 1, a], send.at[e - 1, a], recv.at[e - 1, a], ax.a, t)
        c.start()
        sent.append(c)


def scatter_major(ax, part, rx, recv1, mid, rx2, send2, recv2, sent):
    a, b = ax.a, ax.b

    def column_sum(o):
        total = part[o, b].astype(F32)
        for e in range(1, ax.B):
            slot = rx.at[e - 1, o]
            ax.copy(slot, slot, send2.at[0], recv1.at[e - 1, o], a, b).wait_recv()
            total = total + rx[e - 1, o].astype(F32)
        return total

    for d in range(1, ax.A):
        o = (a + d) % ax.A
        mid[d - 1] = column_sum(o).astype(BF)
        c = ax.copy(mid.at[d - 1], rx2.at[d - 1], send2.at[d - 1], recv2.at[d - 1], o, b)
        c.start()
        sent.append(c)
    total = column_sum(a)
    for d in range(1, ax.A):
        slot = rx2.at[d - 1]
        ax.copy(slot, slot, send2.at[0], recv2.at[d - 1], a, b).wait_recv()
        total = total + rx2[d - 1].astype(F32)
    return total


def body(HA, HB, RA, RB, kvl, UN, NC,
         residual, gain1, wqkv_h, wout_h, cache_h, lengths, cos, sin, gain2, router, routes,
         win_h, wdown_h,
         out, newkv_out,
         wqkv, wout, cache, win, wdown,
         hbuf, rbuf, q8, nkv, o8, hpart, hrx, hmid, hrx2, rpart, rrx, rmid, rrx2, hid, lg,
         wsem, csem,
         hg_s, hg_r, hs_s, hs_r, hs2_s, hs2_r, rg_s, rg_r, rs_s, rs_r, rs2_s, rs2_r):
    T = residual.shape[0]
    R = cache.shape[0]
    E = router.shape[1]
    EL = win.shape[0]
    G = R * kvl // 2
    GC = G // NC
    head = Axis("head", HA, HB)
    req = Axis("req", RA, RB)
    parts = 1 if kvl == 2 else 2

    c_wqkv = pltpu.make_async_copy(wqkv_h, wqkv, wsem.at[0])
    c_wqkv.start()
    def cache_copy(c, s):
        rows = pl.ds(c * GC + s * G, GC)
        return pltpu.make_async_copy(cache_h.at[rows], cache.at[rows], csem.at[c, s])
    for c in range(NC):
        for s in range(parts):
            cache_copy(c, s).start()
    c_wout = pltpu.make_async_copy(wout_h, wout, wsem.at[1])
    c_wout.start()
    c_win = pltpu.make_async_copy(win_h, win, wsem.at[2])
    c_win.start()
    c_wdown = pltpu.make_async_copy(wdown_h, wdown, wsem.at[3])
    c_wdown.start()

    barrier = pltpu.get_barrier_semaphore()
    count = 0
    for ax in (head, req):
        for p in ax.peers():
            pl.semaphore_signal(barrier, inc=1, device_id={ax.name: p}, device_id_type=MESH)
            count += 1

    resid = residual[...].astype(F32)
    hbuf[head.a, head.b] = rms_scale(resid, gain1[...])
    pl.semaphore_wait(barrier, count)

    sent = gather_start(head, hbuf, hg_s, hg_r)
    q8[...] = jnp.zeros_like(q8)
    gather_forward(head, hbuf, hg_s, hg_r, sent)
    for e in range(1, HB):
        gather_column(head, hbuf, hg_s, hg_r, e)
    c_wqkv.wait()
    normed = hbuf[...].reshape(R, D)
    y = jnp.dot(normed, wqkv[...], preferred_element_type=F32)

    C = cos[...]
    S = sin[...]
    lane = lax.broadcasted_iota(jnp.int32, (R, LANES), 1)
    low = (lane & 32) == 0
    zero = jnp.zeros((R, HD), F32)

    def piece(i):
        return y[:, i * HD:(i + 1) * HD]

    def rot(x):
        swapped = jnp.where(low, pltpu.roll(x, LANES - 32, 1), pltpu.roll(x, 32, 1))
        return (x * C + swapped * S).astype(BF).astype(F32)

    for k in range(kvl):
        base = k * (GROUP + 2)
        for g in range(GROUP):
            x = rot(jnp.concatenate([piece(base + g), zero], axis=1)) * (HD ** -0.5)
            if kvl == 2:
                q8[k, pl.ds(k * GROUP + g, G, stride=8), :] = x
            else:
                q8[0, pl.ds(g, G, stride=8), :] = x[:G]
                q8[1, pl.ds(GROUP + g, G, stride=8), :] = x[G:]
        kv = jnp.concatenate([piece(base + GROUP), piece(base + GROUP + 1)], axis=1)
        kv = jnp.where(lane < HD, rot(kv), kv.astype(BF).astype(F32))
        nkv[:, k * LANES:(k + 1) * LANES] = kv
        newkv_out[:, k * LANES:(k + 1) * LANES] = kv.astype(BF)

    position = lax.broadcasted_iota(jnp.int32, (8, cache.shape[2]), 1)
    upper = lax.broadcasted_iota(jnp.int32, (8, cache.shape[2]), 0) >= GROUP

    def attend(first):
        ids = [first + u for u in range(UN)]
        rows8 = [pl.ds(pl.multiple_of(i * 8, 8), 8) for i in ids]
        qs = [jnp.concatenate([q8[0, r, :], q8[1, r, :]], axis=1) for r in rows8]
        if kvl == 2:
            kvs = [jnp.concatenate([cache[i, 0], cache[i, 1]], axis=1) for i in ids]
            nks = [nkv[pl.ds(i, 1), :] for i in ids]
            lens = [lengths[i] for i in ids]
        else:
            kvs = [jnp.concatenate([cache[i, 0], cache[i + G, 0]], axis=1) for i in ids]
            nks = [jnp.concatenate([nkv[pl.ds(i, 1), :], nkv[pl.ds(i + G, 1), :]], axis=1) for i in ids]
            lens = [jnp.where(upper, lengths[i + G], lengths[i]) for i in ids]
        ss = [lax.dot_general(q.astype(BF), kv, (((1,), (1,)), ((), ())), preferred_element_type=F32)
              for q, kv in zip(qs, kvs)]
        owns = [jnp.sum(q * nk, axis=1, keepdims=True) for q, nk in zip(qs, nks)]
        ms = [jnp.where(position < n, s, -1e30) for s, n in zip(ss, lens)]
        peaks = [jnp.maximum(jnp.max(m, axis=1, keepdims=True), o) for m, o in zip(ms, owns)]
        ws = [jnp.exp(m - p) for m, p in zip(ms, peaks)]
        ows = [jnp.exp(o - p) for o, p in zip(owns, peaks)]
        totals = [jnp.sum(w, axis=1, keepdims=True) + o for w, o in zip(ws, ows)]
        os = [jnp.dot(w.astype(BF), kv, preferred_element_type=F32) for w, kv in zip(ws, kvs)]
        for r, o, ow, nk, t in zip(rows8, os, ows, nks, totals):
            o = (o + ow.astype(BF).astype(F32) * nk) / t
            o8[0, r, :] = o[:, :LANES]
            o8[1, r, :] = o[:, LANES:]

    for c in range(NC):
        for s in range(parts):
            cache_copy(c, s).wait()

        @pl.loop(0, GC // UN)
        def _(step):
            attend(c * GC + step * UN)

    heads = []
    for k in range(kvl):
        for g in range(GROUP):
            if kvl == 2:
                z = o8[k, pl.ds(k * GROUP + g, G, stride=8), :]
            else:
                z = jnp.concatenate([o8[0, pl.ds(g, G, stride=8), :],
                                     o8[1, pl.ds(GROUP + g, G, stride=8), :]], axis=0)
            heads.append(z[:, HD:])
    attn = jnp.concatenate(heads, axis=1).astype(BF)
    c_wout.wait()
    attention = jnp.dot(attn, wout[...], preferred_element_type=F32).astype(BF)
    hpart[...] = attention.reshape(HA, HB, T, D)
    for e in range(1, HB):
        scatter_minor(head, hpart, hrx, hs_s, hs_r, e, sent)
    total = scatter_major(head, hpart, hrx, hs_r, hmid, hrx2, hs2_s, hs2_r, sent)
    attended = (resid + total).astype(BF).astype(F32)
    nm = rms_scale(attended, gain2[...])

    lg[...] = jnp.zeros_like(lg)
    lg[:, :E] = jnp.dot(nm, router[...], preferred_element_type=F32)
    logits = lg[...]
    tl = lax.broadcasted_iota(jnp.int32, (T, LANES), 1)
    hit = tl == routes[:, 0:1]
    for j in range(1, routes.shape[1]):
        hit = hit | (tl == routes[:, j:j + 1])
    top = jnp.max(jnp.where(hit, logits, -3e38), axis=1, keepdims=True)
    weight = jnp.where(hit, jnp.exp(jnp.where(hit, logits - top, 0.0)), 0.0)
    gates = weight / jnp.sum(weight, axis=1, keepdims=True)
    high = gates.astype(BF).astype(F32)
    gates = high + pltpu.roll(gates - high, HD, 1)
    rbuf[req.a, req.b, :, :D] = nm
    rbuf[req.a, req.b, :, D:] = gates.astype(BF)

    sent2 = gather_start(req, rbuf, rg_s, rg_r)
    gather_forward(req, rbuf, rg_s, rg_r, sent2)
    c_win.wait()
    c_wdown.wait()
    first = lax.axis_index("req") * EL
    M = RA * T

    def experts(col):
        x = rbuf[:, col, :, :D].reshape(M, D)
        gt = rbuf[:, col, :, D:].reshape(M, LANES).astype(F32)
        gt = gt + pltpu.roll(gt, HD, 1)
        glane = lax.broadcasted_iota(jnp.int32, (M, LANES), 1)

        def up(j, n):
            lo = n * 256
            gate_cols = jnp.dot(x, win[j, :, lo:lo + 256], preferred_element_type=F32)
            up_cols = jnp.dot(x, win[j, :, F + lo:F + lo + 256], preferred_element_type=F32)
            g = jnp.sum(jnp.where(glane == first + j, gt, 0.0), axis=1, keepdims=True)
            act = gate_cols / (1.0 + jnp.exp(-gate_cols)) * up_cols
            hid[j, :, lo:lo + 256] = (act * g).astype(BF)

        @pl.loop(0, EL)
        def _(j):
            for n in range(F // 256):
                up(j, n)

        for n in range(D // 512):
            acc = jnp.zeros((M, 512), F32)
            for j in range(EL):
                acc = acc + jnp.dot(hid[j], wdown[j, :, n * 512:(n + 1) * 512],
                                    preferred_element_type=F32)
            rpart[:, col, :, n * 512:(n + 1) * 512] = acc.astype(BF).reshape(RA, T, 512)

    experts(req.b)
    for e in range(1, RB):
        o = gather_column(req, rbuf, rg_s, rg_r, e)
        experts(o)
        scatter_minor(req, rpart, rrx, rs_s, rs_r, RB - e, sent2)
    mixed = scatter_major(req, rpart, rrx, rs_r, rmid, rrx2, rs2_s, rs2_r, sent2)
    out[...] = (attended + mixed).astype(BF)
    for c in sent + sent2:
        c.wait_send()


def local(head_n, req_n, residual_in, attn_gain, w_qkv, w_out, kv_cache, lengths,
          moe_gain, w_router, routes, w_in, w_down):
    T = residual_in.shape[0]
    R, kvl, L = kv_cache.shape[:3]
    E = w_router.shape[1]
    EL = w_in.shape[0]
    HB = 2 if head_n % 2 == 0 else 1
    HA = head_n // HB
    RA = 4 if req_n % 4 == 0 else 1
    RB = req_n // RA
    G = R * kvl // 2
    UN, NC = 8, 4
    index = jnp.arange(HD // 2).astype(F32)
    frequency = jnp.power(THETA, -2.0 * index / HD)
    angle = lengths.astype(F32)[:, None] * frequency[None, :]
    c, s = jnp.cos(angle), jnp.sin(angle)
    cos = jnp.concatenate([c, c, c, c], axis=1)
    sin = jnp.concatenate([-s, s, -s, s], axis=1)
    vm = pl.BlockSpec(memory_space=pltpu.VMEM)
    sm = pl.BlockSpec(memory_space=pltpu.SMEM)
    hbm = pl.BlockSpec(memory_space=pl.ANY)
    dma = pltpu.SemaphoreType.DMA
    V = pltpu.VMEM
    mn = lambda n: max(n, 1)
    layer_out, new_kv = pl.pallas_call(
        functools.partial(body, HA, HB, RA, RB, kvl, UN, NC),
        out_shape=(jax.ShapeDtypeStruct((T, D), BF),
                   jax.ShapeDtypeStruct((R, kvl * LANES), BF)),
        in_specs=[vm, vm, hbm, hbm, hbm, sm, vm, vm, vm, vm, vm, hbm, hbm],
        out_specs=(vm, vm),
        scratch_shapes=[
            V((D, kvl * (GROUP + 2) * HD), BF), V(w_out.shape, BF), V(kv_cache.shape, BF),
            V(w_in.shape, BF), V(w_down.shape, BF),
            V((HA, HB, T, D), BF), V((RA, RB, T, WIDE), BF),
            V((2, G * 8, LANES), F32), V((R, kvl * LANES), F32), V((2, G * 8, LANES), F32),
            V((HA, HB, T, D), BF), V((mn(HB - 1), HA, T, D), BF),
            V((mn(HA - 1), T, D), BF), V((mn(HA - 1), T, D), BF),
            V((RA, RB, T, D), BF), V((mn(RB - 1), RA, T, D), BF),
            V((mn(RA - 1), T, D), BF), V((mn(RA - 1), T, D), BF),
            V((EL, RA * T, F), BF), V((T, LANES), F32),
            dma((4,)), dma((NC, 2)),
            dma((HA, HB)), dma((HA, HB)), dma((mn(HB - 1), HA)), dma((mn(HB - 1), HA)),
            dma((mn(HA - 1),)), dma((mn(HA - 1),)),
            dma((RA, RB)), dma((RA, RB)), dma((mn(RB - 1), RA)), dma((mn(RB - 1), RA)),
            dma((mn(RA - 1),)), dma((mn(RA - 1),)),
        ],
        compiler_params=pltpu.CompilerParams(
            collective_id=0, has_side_effects=True, vmem_limit_bytes=56 << 20),
        name="layer",
    )(residual_in, attn_gain.reshape(1, D), w_qkv.reshape(D, kvl * (GROUP + 2) * HD), w_out,
      kv_cache, lengths, cos, sin, moe_gain.reshape(1, D), w_router, routes, w_in, w_down)
    return layer_out, new_kv.reshape(R, kvl, LANES)


def solution(mesh):
    return jax.shard_map(
        functools.partial(local, mesh.shape["head"], mesh.shape["req"]),
        mesh=mesh,
        in_specs=(
            P(("req", "head"), None),
            P(),
            P(None, "head", None),
            P("head", None),
            P("req", "head", None, None),
            P("req"),
            P(),
            P(),
            P(("req", "head"), None),
            P("req", None, None),
            P("req", None, None),
        ),
        out_specs=(P(("req", "head"), None), P("req", "head", None)),
        check_vma=False,
    )
```

```python
import functools

import jax
import jax.numpy as jnp
import numpy as np
from jax import lax
from jax.experimental import pallas as pl
from jax.experimental.pallas import tpu as pltpu
from jax.sharding import PartitionSpec as P

D = 1536
HEADS = 24
KV = 8
HD = 64
F = 512
GROUP = HEADS // KV
LANES = 128
WIDE = D + LANES

EPSILON = 1e-06
THETA = 10000.0
CHUNKS = 2
MESH = pl.DeviceIdType.MESH
BF = jnp.bfloat16
F32 = jnp.float32


def rms_scale(wide, gain):
    mean_square = jnp.mean(wide * wide, axis=-1, keepdims=True)
    return (wide * lax.rsqrt(mean_square + EPSILON) * gain.astype(F32)).astype(BF)


def row(ref):
    wide = ref[...].astype(F32)
    return jnp.concatenate([wide[i:i + 1] for i in range(wide.shape[0])], axis=1)


def dot_nt(a, b):
    return lax.dot_general(a, b, (((1,), (1,)), ((), ())), preferred_element_type=F32)


def eye(n):
    same = lax.broadcasted_iota(jnp.int32, (n, n), 0) == lax.broadcasted_iota(jnp.int32, (n, n), 1)
    return jnp.where(same, 1.0, 0.0).astype(BF)


class Axis:
    def __init__(self, name, A, B):
        self.name, self.A, self.B = name, A, B
        me = lax.axis_index(name)
        self.a, self.b = me // B, me % B

    def peers(self):
        A, B = self.A, self.B
        out = [((self.a + d) % A) * B + self.b for d in range(1, A)]
        return out + [self.a * B + (self.b + d) % B for d in range(1, B)]

    def copy(self, src, dst, send, recv, a, b):
        return pltpu.make_async_remote_copy(
            src_ref=src, dst_ref=dst, send_sem=send, recv_sem=recv,
            device_id={self.name: a * self.B + b}, device_id_type=MESH)


def chunk(buf, o, p, c):
    rows = buf.shape[2] // CHUNKS
    return buf.at[o, p, pl.ds(c * rows, rows)]


def gather_start(ax, buf, send, recv):
    sent = []
    a, b = ax.a, ax.b
    for c in range(CHUNKS):
        own = chunk(buf, a, b, c)
        if ax.A > 1:
            sent.append(ax.copy(own, own, send.at[0, 0, c], recv.at[a, b, c], (a + 1) % ax.A, b))
            sent[-1].start()
        for d in range(1, ax.B):
            sent.append(ax.copy(own, own, send.at[0, d, c], recv.at[a, b, c], a, (b + d) % ax.B))
            sent[-1].start()
    return sent


def gather_forward(ax, buf, send, recv, sent):
    a, b = ax.a, ax.b
    for d in range(1, ax.A):
        o = (a + ax.A - d) % ax.A
        for c in range(CHUNKS):
            block = chunk(buf, o, b, c)
            ax.copy(block, block, send.at[0, 0, c], recv.at[o, b, c], a, b).wait_recv()
            if d < ax.A - 1:
                sent.append(ax.copy(block, block, send.at[d, 0, c], recv.at[o, b, c],
                                    (a + 1) % ax.A, b))
                sent[-1].start()
            for e in range(1, ax.B):
                sent.append(ax.copy(block, block, send.at[d, e, c], recv.at[o, b, c],
                                    a, (b + e) % ax.B))
                sent[-1].start()


def gather_column(ax, buf, send, recv, e):
    o = (ax.b + ax.B - e) % ax.B
    for d in range(ax.A):
        a = (ax.a + ax.A - d) % ax.A
        for c in range(CHUNKS):
            block = chunk(buf, a, o, c)
            ax.copy(block, block, send.at[0, 0, c], recv.at[a, o, c], ax.a, ax.b).wait_recv()
    return o


def scatter_minor(ax, part, rx, send, recv, e, sent):
    t = (ax.b + e) % ax.B
    for d in range(1, ax.A + 1):
        a = (ax.a + d) % ax.A
        c = ax.copy(part.at[a, t], rx.at[e - 1, a], send.at[e - 1, a], recv.at[e - 1, a], ax.a, t)
        c.start()
        sent.append(c)


def scatter_major(ax, part, rx, recv1, mid, rx2, send2, recv2, sent):
    a, b = ax.a, ax.b

    def column_sum(o):
        total = part[o, b].astype(F32)
        for e in range(1, ax.B):
            slot = rx.at[e - 1, o]
            ax.copy(slot, slot, send2.at[0], recv1.at[e - 1, o], a, b).wait_recv()
            total = total + rx[e - 1, o].astype(F32)
        return total

    for d in range(1, ax.A):
        o = (a + d) % ax.A
        mid[d - 1] = column_sum(o).astype(BF)
        c = ax.copy(mid.at[d - 1], rx2.at[d - 1], send2.at[d - 1], recv2.at[d - 1], o, b)
        c.start()
        sent.append(c)
    total = column_sum(a)
    for d in range(1, ax.A):
        slot = rx2.at[d - 1]
        ax.copy(slot, slot, send2.at[0], recv2.at[d - 1], a, b).wait_recv()
        total = total + rx2[d - 1].astype(F32)
    return total


def body(HA, HB, RA, RB, kvl, UN, NC,
         residual, gain1, wqkv_h, wout_h, cache_h, lengths, lenrow, freq, gain2, router, routes,
         win_h, wdown_h,
         out, newkv_out,
         wqkv, wout, cache, win, wdown,
         hbuf, rbuf, q8, nkv, o8, hpart, hrx, hmid, hrx2, rpart, rrx, rmid, rrx2, hid, lg, hits,
         wsem, csem,
         hg_s, hg_r, hs_s, hs_r, hs2_s, hs2_r, rg_s, rg_r, rs_s, rs_r, rs2_s, rs2_r):
    T = residual.shape[0]
    R = cache.shape[0]
    E = router.shape[0]
    EL = win.shape[0]
    G = R * kvl // 2
    GC = G // NC
    head = Axis("head", HA, HB)
    req = Axis("req", RA, RB)
    parts = 1 if kvl == 2 else 2

    c_wqkv = pltpu.make_async_copy(wqkv_h, wqkv, wsem.at[0])
    c_wqkv.start()
    def cache_copy(c, s):
        rows = pl.ds(c * GC + s * G, GC)
        return pltpu.make_async_copy(cache_h.at[rows], cache.at[rows], csem.at[c, s])
    for c in range(NC):
        for s in range(parts):
            cache_copy(c, s).start()
    c_wout = pltpu.make_async_copy(wout_h, wout, wsem.at[1])
    c_wout.start()
    c_win = pltpu.make_async_copy(win_h, win, wsem.at[2])
    c_win.start()
    c_wdown = pltpu.make_async_copy(wdown_h, wdown, wsem.at[3])
    c_wdown.start()

    barrier = pltpu.get_barrier_semaphore()
    count = 0
    for ax in (head, req):
        for p in ax.peers():
            pl.semaphore_signal(barrier, inc=1, device_id={ax.name: p}, device_id_type=MESH)
            count += 1

    resid = residual[...].astype(F32)
    hbuf[head.a, head.b] = rms_scale(resid, row(gain1))
    pl.semaphore_wait(barrier, count)

    sent = gather_start(head, hbuf, hg_s, hg_r)
    q8[...] = jnp.zeros_like(q8)
    lane = lax.broadcasted_iota(jnp.int32, (R, LANES), 1)
    low = (lane & 32) == 0
    column = dot_nt(eye(R), jnp.broadcast_to(lenrow[...].astype(F32), (LANES, R)).astype(BF))
    angle = column * freq[...]
    C = jnp.cos(angle)
    S = jnp.sin(angle)
    S = jnp.where(low, -S, S)
    expert = lax.broadcasted_iota(jnp.int32, (LANES, T), 0)
    hit = expert == routes[0:1, :]
    for j in range(1, routes.shape[0]):
        hit = hit | (expert == routes[j:j + 1, :])
    hits[...] = dot_nt(eye(T), jnp.where(hit, 1.0, 0.0).astype(BF))
    gather_forward(head, hbuf, hg_s, hg_r, sent)
    for e in range(1, HB):
        gather_column(head, hbuf, hg_s, hg_r, e)
    c_wqkv.wait()
    normed = hbuf[...].reshape(R, D)
    y = dot_nt(normed, wqkv[...])

    zero = jnp.zeros((R, HD), F32)

    def piece(i):
        return y[:, i * HD:(i + 1) * HD]

    def rot(x):
        swapped = jnp.where(low, pltpu.roll(x, LANES - 32, 1), pltpu.roll(x, 32, 1))
        return (x * C + swapped * S).astype(BF).astype(F32)

    for k in range(kvl):
        base = k * (GROUP + 2)
        for g in range(GROUP):
            x = rot(jnp.concatenate([piece(base + g), zero], axis=1)) * (HD ** -0.5)
            if kvl == 2:
                q8[k, pl.ds(k * GROUP + g, G, stride=8), :] = x
            else:
                q8[0, pl.ds(g, G, stride=8), :] = x[:G]
                q8[1, pl.ds(GROUP + g, G, stride=8), :] = x[G:]
        kv = jnp.concatenate([piece(base + GROUP), piece(base + GROUP + 1)], axis=1)
        kv = jnp.where(lane < HD, rot(kv), kv.astype(BF).astype(F32))
        nkv[:, k * LANES:(k + 1) * LANES] = kv
        newkv_out[:, k, :] = kv.astype(BF)

    position = lax.broadcasted_iota(jnp.int32, (8, cache.shape[2]), 1)
    upper = lax.broadcasted_iota(jnp.int32, (8, cache.shape[2]), 0) >= GROUP

    def attend(first):
        ids = [first + u for u in range(UN)]
        rows8 = [pl.ds(pl.multiple_of(i * 8, 8), 8) for i in ids]
        qs = [jnp.concatenate([q8[0, r, :], q8[1, r, :]], axis=1) for r in rows8]
        if kvl == 2:
            kvs = [jnp.concatenate([cache[i, 0], cache[i, 1]], axis=1) for i in ids]
            nks = [nkv[pl.ds(i, 1), :] for i in ids]
            lens = [lengths[i] for i in ids]
        else:
            kvs = [jnp.concatenate([cache[i, 0], cache[i + G, 0]], axis=1) for i in ids]
            nks = [jnp.concatenate([nkv[pl.ds(i, 1), :], nkv[pl.ds(i + G, 1), :]], axis=1) for i in ids]
            lens = [jnp.where(upper, lengths[i + G], lengths[i]) for i in ids]
        ss = [dot_nt(q.astype(BF), kv) for q, kv in zip(qs, kvs)]
        owns = [jnp.sum(q * nk, axis=1, keepdims=True) for q, nk in zip(qs, nks)]
        ms = [jnp.where(position < n, s, -1e30) for s, n in zip(ss, lens)]
        peaks = [jnp.maximum(jnp.max(m, axis=1, keepdims=True), o) for m, o in zip(ms, owns)]
        ws = [jnp.exp(m - p) for m, p in zip(ms, peaks)]
        ows = [jnp.exp(o - p) for o, p in zip(owns, peaks)]
        totals = [jnp.sum(w, axis=1, keepdims=True) + o for w, o in zip(ws, ows)]
        os = [jnp.dot(w.astype(BF), kv, preferred_element_type=F32) for w, kv in zip(ws, kvs)]
        for r, o, ow, nk, t in zip(rows8, os, ows, nks, totals):
            o = (o + ow.astype(BF).astype(F32) * nk) / t
            o8[0, r, :] = o[:, :LANES]
            o8[1, r, :] = o[:, LANES:]

    for c in range(NC):
        for s in range(parts):
            cache_copy(c, s).wait()

        @pl.loop(0, GC // UN)
        def _(step):
            attend(c * GC + step * UN)

    heads = []
    for k in range(kvl):
        for g in range(GROUP):
            if kvl == 2:
                z = o8[k, pl.ds(k * GROUP + g, G, stride=8), :]
            else:
                z = jnp.concatenate([o8[0, pl.ds(g, G, stride=8), :],
                                     o8[1, pl.ds(GROUP + g, G, stride=8), :]], axis=0)
            heads.append(z[:, HD:])
    attn = jnp.concatenate(heads, axis=1).astype(BF)
    c_wout.wait()
    attention = jnp.dot(attn, wout[...], preferred_element_type=F32).astype(BF)
    hpart[...] = attention.reshape(HA, HB, T, D)
    for e in range(1, HB):
        scatter_minor(head, hpart, hrx, hs_s, hs_r, e, sent)
    total = scatter_major(head, hpart, hrx, hs_r, hmid, hrx2, hs2_s, hs2_r, sent)
    attended = (resid + total).astype(BF).astype(F32)
    nm = rms_scale(attended, row(gain2))

    lg[...] = jnp.zeros_like(lg)
    lg[:, :E] = dot_nt(nm, router[...])
    logits = lg[...]
    hit = hits[...] > 0.5
    top = jnp.max(jnp.where(hit, logits, -3e38), axis=1, keepdims=True)
    weight = jnp.where(hit, jnp.exp(jnp.where(hit, logits - top, 0.0)), 0.0)
    gates = weight / jnp.sum(weight, axis=1, keepdims=True)
    high = gates.astype(BF).astype(F32)
    gates = high + pltpu.roll(gates - high, HD, 1)
    rbuf[req.a, req.b, :, :D] = nm
    rbuf[req.a, req.b, :, D:] = gates.astype(BF)

    sent2 = gather_start(req, rbuf, rg_s, rg_r)
    gather_forward(req, rbuf, rg_s, rg_r, sent2)
    c_win.wait()
    c_wdown.wait()
    first = lax.axis_index("req") * EL
    M = RA * T

    def experts(col):
        x = rbuf[:, col, :, :D].reshape(M, D)
        gt = rbuf[:, col, :, D:].reshape(M, LANES).astype(F32)
        gt = gt + pltpu.roll(gt, HD, 1)
        glane = lax.broadcasted_iota(jnp.int32, (M, LANES), 1)

        def up(j, n):
            lo = n * 256
            gate_cols = jnp.dot(x, win[j, :, lo:lo + 256], preferred_element_type=F32)
            up_cols = jnp.dot(x, win[j, :, F + lo:F + lo + 256], preferred_element_type=F32)
            g = jnp.sum(jnp.where(glane == first + j, gt, 0.0), axis=1, keepdims=True)
            act = gate_cols / (1.0 + jnp.exp(-gate_cols)) * up_cols
            hid[j, :, lo:lo + 256] = (act * g).astype(BF)

        @pl.loop(0, EL)
        def _(j):
            for n in range(F // 256):
                up(j, n)

        for n in range(D // 512):
            acc = jnp.zeros((M, 512), F32)
            for j in range(EL):
                acc = acc + jnp.dot(hid[j], wdown[j, :, n * 512:(n + 1) * 512],
                                    preferred_element_type=F32)
            rpart[:, col, :, n * 512:(n + 1) * 512] = acc.astype(BF).reshape(RA, T, 512)

    experts(req.b)
    for e in range(1, RB):
        o = gather_column(req, rbuf, rg_s, rg_r, e)
        experts(o)
        scatter_minor(req, rpart, rrx, rs_s, rs_r, RB - e, sent2)
    mixed = scatter_major(req, rpart, rrx, rs_r, rmid, rrx2, rs2_s, rs2_r, sent2)
    out[...] = (attended + mixed).astype(BF)
    for c in sent + sent2:
        c.wait_send()


def pinned(*arrays):
    return [a if i == 5 else pltpu.with_memory_space_constraint(a, pltpu.HBM)
            for i, a in enumerate(arrays)]


def local(head_n, req_n, residual_in, attn_gain, w_qkv, w_out, kv_cache, lengths,
          moe_gain, w_router, routes, w_in, w_down):
    T = residual_in.shape[0]
    R, kvl, L = kv_cache.shape[:3]
    E = w_router.shape[1]
    EL = w_in.shape[0]
    HB = 2 if head_n % 2 == 0 else 1
    HA = head_n // HB
    RA = 4 if req_n % 4 == 0 else 1
    RB = req_n // RA
    G = R * kvl // 2
    UN, NC = 8, 4
    index = np.arange(HD // 2)
    freq = np.power(THETA, -2.0 * index / HD).astype(np.float32)
    freq = np.tile(freq, 4).reshape(1, LANES)
    vm = pl.BlockSpec(memory_space=pltpu.VMEM)
    sm = pl.BlockSpec(memory_space=pltpu.SMEM)
    hbm = pl.BlockSpec(memory_space=pltpu.HBM)
    dma = pltpu.SemaphoreType.DMA
    V = pltpu.VMEM
    mn = lambda n: max(n, 1)
    layer_out, new_kv = pl.pallas_call(
        functools.partial(body, HA, HB, RA, RB, kvl, UN, NC),
        out_shape=(jax.ShapeDtypeStruct((T, D), BF),
                   jax.ShapeDtypeStruct((R, kvl, LANES), BF)),
        in_specs=[vm, vm, hbm, hbm, hbm, sm, vm, vm, vm, vm, vm, hbm, hbm],
        out_specs=(vm, vm),
        scratch_shapes=[
            V((kvl * (GROUP + 2) * HD, D), BF), V(w_out.shape, BF), V(kv_cache.shape, BF),
            V(w_in.shape, BF), V(w_down.shape, BF),
            V((HA, HB, T, D), BF), V((RA, RB, T, WIDE), BF),
            V((2, G * 8, LANES), F32), V((R, kvl * LANES), F32), V((2, G * 8, LANES), F32),
            V((HA, HB, T, D), BF), V((mn(HB - 1), HA, T, D), BF),
            V((mn(HA - 1), T, D), BF), V((mn(HA - 1), T, D), BF),
            V((RA, RB, T, D), BF), V((mn(RB - 1), RA, T, D), BF),
            V((mn(RA - 1), T, D), BF), V((mn(RA - 1), T, D), BF),
            V((EL, RA * T, F), BF), V((T, LANES), F32), V((T, LANES), F32),
            dma((4,)), dma((NC, 2)),
            dma((HA, HB, CHUNKS)), dma((HA, HB, CHUNKS)), dma((mn(HB - 1), HA)), dma((mn(HB - 1), HA)),
            dma((mn(HA - 1),)), dma((mn(HA - 1),)),
            dma((RA, RB, CHUNKS)), dma((RA, RB, CHUNKS)), dma((mn(RB - 1), RA)), dma((mn(RB - 1), RA)),
            dma((mn(RA - 1),)), dma((mn(RA - 1),)),
        ],
        compiler_params=pltpu.CompilerParams(
            collective_id=0, has_side_effects=True, vmem_limit_bytes=44 << 20),
        name="layer",
    )(*pinned(residual_in, attn_gain.reshape(D // LANES, LANES),
      w_qkv.transpose(1, 2, 0).reshape(kvl * (GROUP + 2) * HD, D), w_out,
      kv_cache, lengths, lengths.reshape(1, R), freq, moe_gain.reshape(D // LANES, LANES),
      w_router.T, routes.T, w_in, w_down))
    return layer_out, new_kv


def solution(mesh):
    return jax.shard_map(
        functools.partial(local, mesh.shape["head"], mesh.shape["req"]),
        mesh=mesh,
        in_specs=(
            P(("req", "head"), None),
            P(),
            P(None, "head", None),
            P("head", None),
            P("req", "head", None, None),
            P("req"),
            P(),
            P(),
            P(("req", "head"), None),
            P("req", None, None),
            P("req", None, None),
        ),
        out_specs=(P(("req", "head"), None), P("req", "head", None)),
        check_vma=False,
    )
```

```python
import functools

import jax
import jax.numpy as jnp
import numpy as np
from jax import lax
from jax.experimental import pallas as pl
from jax.experimental.pallas import tpu as pltpu
from jax.sharding import PartitionSpec as P

D = 1536
HEADS = 24
KV = 8
HD = 64
F = 512
GROUP = HEADS // KV
LANES = 128
WIDE = D + LANES

EPSILON = 1e-06
THETA = 10000.0
CHUNKS = 2
MESH = pl.DeviceIdType.MESH
BF = jnp.bfloat16
F32 = jnp.float32


def rms_scale(wide, gain):
    mean_square = jnp.mean(wide * wide, axis=-1, keepdims=True)
    return (wide * lax.rsqrt(mean_square + EPSILON) * gain.astype(F32)).astype(BF)


def row(ref):
    wide = ref[...].astype(F32)
    return jnp.concatenate([wide[i:i + 1] for i in range(wide.shape[0])], axis=1)


def dot_nt(a, b):
    return lax.dot_general(a, b, (((1,), (1,)), ((), ())), preferred_element_type=F32)


def eye(n):
    same = lax.broadcasted_iota(jnp.int32, (n, n), 0) == lax.broadcasted_iota(jnp.int32, (n, n), 1)
    return jnp.where(same, 1.0, 0.0).astype(BF)


class Axis:
    def __init__(self, name, A, B):
        self.name, self.A, self.B = name, A, B
        me = lax.axis_index(name)
        self.a, self.b = me // B, me % B

    def peers(self):
        A, B = self.A, self.B
        out = [((self.a + d) % A) * B + self.b for d in range(1, A)]
        return out + [self.a * B + (self.b + d) % B for d in range(1, B)]

    def copy(self, src, dst, send, recv, a, b):
        return pltpu.make_async_remote_copy(
            src_ref=src, dst_ref=dst, send_sem=send, recv_sem=recv,
            device_id={self.name: a * self.B + b}, device_id_type=MESH)


def chunk(buf, o, p, c):
    rows = buf.shape[2] // CHUNKS
    return buf.at[o, p, pl.ds(c * rows, rows)]


def gather_start(ax, buf, send, recv):
    sent = []
    a, b = ax.a, ax.b
    for c in range(CHUNKS):
        own = chunk(buf, a, b, c)
        if ax.A > 1:
            sent.append(ax.copy(own, own, send.at[0, 0, c], recv.at[a, b, c], (a + 1) % ax.A, b))
            sent[-1].start()
        for d in range(1, ax.B):
            sent.append(ax.copy(own, own, send.at[0, d, c], recv.at[a, b, c], a, (b + d) % ax.B))
            sent[-1].start()
    return sent


def gather_forward(ax, buf, send, recv, sent):
    a, b = ax.a, ax.b
    for d in range(1, ax.A):
        o = (a + ax.A - d) % ax.A
        for c in range(CHUNKS):
            block = chunk(buf, o, b, c)
            ax.copy(block, block, send.at[0, 0, c], recv.at[o, b, c], a, b).wait_recv()
            if d < ax.A - 1:
                sent.append(ax.copy(block, block, send.at[d, 0, c], recv.at[o, b, c],
                                    (a + 1) % ax.A, b))
                sent[-1].start()
            for e in range(1, ax.B):
                sent.append(ax.copy(block, block, send.at[d, e, c], recv.at[o, b, c],
                                    a, (b + e) % ax.B))
                sent[-1].start()


def gather_column(ax, buf, send, recv, e):
    o = (ax.b + ax.B - e) % ax.B
    for d in range(ax.A):
        a = (ax.a + ax.A - d) % ax.A
        for c in range(CHUNKS):
            block = chunk(buf, a, o, c)
            ax.copy(block, block, send.at[0, 0, c], recv.at[a, o, c], ax.a, ax.b).wait_recv()
    return o


def scatter_minor(ax, part, rx, send, recv, e, sent):
    t = (ax.b + e) % ax.B
    rows = part.shape[2] // CHUNKS
    for d in range(1, ax.A + 1):
        a = (ax.a + d) % ax.A
        for c in range(CHUNKS):
            sent.append(ax.copy(chunk(part, a, t, c), rx.at[e - 1, a, pl.ds(c * rows, rows)],
                                send.at[e - 1, a, c], recv.at[e - 1, a, c], ax.a, t))
            sent[-1].start()


def scatter_major(ax, part, rx, recv1, mid, rx2, send2, recv2, sent):
    a, b = ax.a, ax.b
    rows = part.shape[2] // CHUNKS

    def column_sum(o, c):
        span = pl.ds(c * rows, rows)
        total = part[o, b, span].astype(F32)
        for e in range(1, ax.B):
            slot = rx.at[e - 1, o, span]
            ax.copy(slot, slot, send2.at[0, 0], recv1.at[e - 1, o, c], a, b).wait_recv()
            total = total + rx[e - 1, o, span].astype(F32)
        return total

    for d in range(1, ax.A):
        o = (a + d) % ax.A
        for c in range(CHUNKS):
            span = pl.ds(c * rows, rows)
            mid[d - 1, span] = column_sum(o, c).astype(BF)
            sent.append(ax.copy(mid.at[d - 1, span], rx2.at[d - 1, span],
                                send2.at[d - 1, c], recv2.at[d - 1, c], o, b))
            sent[-1].start()
    totals = [column_sum(a, c) for c in range(CHUNKS)]
    for d in range(1, ax.A):
        for c in range(CHUNKS):
            span = pl.ds(c * rows, rows)
            slot = rx2.at[d - 1, span]
            ax.copy(slot, slot, send2.at[0, 0], recv2.at[d - 1, c], a, b).wait_recv()
            totals[c] = totals[c] + rx2[d - 1, span].astype(F32)
    return jnp.concatenate(totals, axis=0)


def body(HA, HB, RA, RB, kvl, UN, NC,
         residual, gain1, wqkv_h, wout_h, cache_h, lengths, lenrow, freq, gain2, router, routes,
         win_h, wdown_h,
         out, newkv_out,
         wqkv, wout, cache, win, wdown,
         hbuf, rbuf, q8, nkv, o8, hpart, hrx, hmid, hrx2, rpart, rrx, rmid, rrx2, hid, lg, hits,
         wsem, csem,
         hg_s, hg_r, hs_s, hs_r, hs2_s, hs2_r, rg_s, rg_r, rs_s, rs_r, rs2_s, rs2_r):
    T = residual.shape[0]
    R = cache.shape[0]
    E = router.shape[0]
    EL = win.shape[0]
    G = R * kvl // 2
    GC = G // NC
    head = Axis("head", HA, HB)
    req = Axis("req", RA, RB)
    parts = 1 if kvl == 2 else 2

    c_wqkv = pltpu.make_async_copy(wqkv_h, wqkv, wsem.at[0])
    c_wqkv.start()
    def cache_copy(c, s):
        rows = pl.ds(c * GC + s * G, GC)
        return pltpu.make_async_copy(cache_h.at[rows], cache.at[rows], csem.at[c, s])
    for c in range(NC):
        for s in range(parts):
            cache_copy(c, s).start()
    c_wout = pltpu.make_async_copy(wout_h, wout, wsem.at[1])
    c_wout.start()
    c_win = pltpu.make_async_copy(win_h, win, wsem.at[2])
    c_win.start()
    c_wdown = pltpu.make_async_copy(wdown_h, wdown, wsem.at[3])
    c_wdown.start()

    barrier = pltpu.get_barrier_semaphore()
    count = 0
    for ax in (head, req):
        for p in ax.peers():
            pl.semaphore_signal(barrier, inc=1, device_id={ax.name: p}, device_id_type=MESH)
            count += 1

    resid = residual[...].astype(F32)
    hbuf[head.a, head.b] = rms_scale(resid, row(gain1))
    pl.semaphore_wait(barrier, count)

    sent = gather_start(head, hbuf, hg_s, hg_r)
    q8[...] = jnp.zeros_like(q8)
    lane = lax.broadcasted_iota(jnp.int32, (R, LANES), 1)
    low = (lane & 32) == 0
    column = dot_nt(eye(R), jnp.broadcast_to(lenrow[...].astype(F32), (LANES, R)).astype(BF))
    angle = column * freq[...]
    C = jnp.cos(angle)
    S = jnp.sin(angle)
    S = jnp.where(low, -S, S)
    expert = lax.broadcasted_iota(jnp.int32, (LANES, T), 0)
    hit = expert == routes[0:1, :]
    for j in range(1, routes.shape[0]):
        hit = hit | (expert == routes[j:j + 1, :])
    hits[...] = dot_nt(eye(T), jnp.where(hit, 1.0, 0.0).astype(BF))
    gather_forward(head, hbuf, hg_s, hg_r, sent)
    for e in range(1, HB):
        gather_column(head, hbuf, hg_s, hg_r, e)
    c_wqkv.wait()
    normed = hbuf[...].reshape(R, D)
    y = dot_nt(normed, wqkv[...])

    zero = jnp.zeros((R, HD), F32)

    def piece(i):
        return y[:, i * HD:(i + 1) * HD]

    def rot(x):
        swapped = jnp.where(low, pltpu.roll(x, LANES - 32, 1), pltpu.roll(x, 32, 1))
        return (x * C + swapped * S).astype(BF).astype(F32)

    for k in range(kvl):
        base = k * (GROUP + 2)
        for g in range(GROUP):
            x = rot(jnp.concatenate([piece(base + g), zero], axis=1)) * (HD ** -0.5)
            if kvl == 2:
                q8[k, pl.ds(k * GROUP + g, G, stride=8), :] = x
            else:
                q8[0, pl.ds(g, G, stride=8), :] = x[:G]
                q8[1, pl.ds(GROUP + g, G, stride=8), :] = x[G:]
        kv = jnp.concatenate([piece(base + GROUP), piece(base + GROUP + 1)], axis=1)
        kv = jnp.where(lane < HD, rot(kv), kv.astype(BF).astype(F32))
        nkv[:, k * LANES:(k + 1) * LANES] = kv
        newkv_out[:, k, :] = kv.astype(BF)

    position = lax.broadcasted_iota(jnp.int32, (8, cache.shape[2]), 1)
    upper = lax.broadcasted_iota(jnp.int32, (8, cache.shape[2]), 0) >= GROUP

    def attend(first):
        ids = [first + u for u in range(UN)]
        rows8 = [pl.ds(pl.multiple_of(i * 8, 8), 8) for i in ids]
        qs = [jnp.concatenate([q8[0, r, :], q8[1, r, :]], axis=1) for r in rows8]
        if kvl == 2:
            kvs = [jnp.concatenate([cache[i, 0], cache[i, 1]], axis=1) for i in ids]
            nks = [nkv[pl.ds(i, 1), :] for i in ids]
            lens = [lengths[i] for i in ids]
        else:
            kvs = [jnp.concatenate([cache[i, 0], cache[i + G, 0]], axis=1) for i in ids]
            nks = [jnp.concatenate([nkv[pl.ds(i, 1), :], nkv[pl.ds(i + G, 1), :]], axis=1) for i in ids]
            lens = [jnp.where(upper, lengths[i + G], lengths[i]) for i in ids]
        ss = [dot_nt(q.astype(BF), kv) for q, kv in zip(qs, kvs)]
        owns = [jnp.sum(q * nk, axis=1, keepdims=True) for q, nk in zip(qs, nks)]
        ms = [jnp.where(position < n, s, -1e30) for s, n in zip(ss, lens)]
        peaks = [jnp.maximum(jnp.max(m, axis=1, keepdims=True), o) for m, o in zip(ms, owns)]
        ws = [jnp.exp(m - p) for m, p in zip(ms, peaks)]
        ows = [jnp.exp(o - p) for o, p in zip(owns, peaks)]
        totals = [jnp.sum(w, axis=1, keepdims=True) + o for w, o in zip(ws, ows)]
        os = [jnp.dot(w.astype(BF), kv, preferred_element_type=F32) for w, kv in zip(ws, kvs)]
        for r, o, ow, nk, t in zip(rows8, os, ows, nks, totals):
            o = (o + ow.astype(BF).astype(F32) * nk) / t
            o8[0, r, :] = o[:, :LANES]
            o8[1, r, :] = o[:, LANES:]

    for c in range(NC):
        for s in range(parts):
            cache_copy(c, s).wait()

        @pl.loop(0, GC // UN)
        def _(step):
            attend(c * GC + step * UN)

    heads = []
    for k in range(kvl):
        for g in range(GROUP):
            if kvl == 2:
                z = o8[k, pl.ds(k * GROUP + g, G, stride=8), :]
            else:
                z = jnp.concatenate([o8[0, pl.ds(g, G, stride=8), :],
                                     o8[1, pl.ds(GROUP + g, G, stride=8), :]], axis=0)
            heads.append(z[:, HD:])
    attn = jnp.concatenate(heads, axis=1).astype(BF)
    c_wout.wait()
    attention = jnp.dot(attn, wout[...], preferred_element_type=F32).astype(BF)
    hpart[...] = attention.reshape(HA, HB, T, D)
    for e in range(1, HB):
        scatter_minor(head, hpart, hrx, hs_s, hs_r, e, sent)
    total = scatter_major(head, hpart, hrx, hs_r, hmid, hrx2, hs2_s, hs2_r, sent)
    attended = (resid + total).astype(BF).astype(F32)
    nm = rms_scale(attended, row(gain2))

    lg[...] = jnp.zeros_like(lg)
    lg[:, :E] = dot_nt(nm, router[...])
    logits = lg[...]
    hit = hits[...] > 0.5
    top = jnp.max(jnp.where(hit, logits, -3e38), axis=1, keepdims=True)
    weight = jnp.where(hit, jnp.exp(jnp.where(hit, logits - top, 0.0)), 0.0)
    gates = weight / jnp.sum(weight, axis=1, keepdims=True)
    high = gates.astype(BF).astype(F32)
    gates = high + pltpu.roll(gates - high, HD, 1)
    rbuf[req.a, req.b, :, :D] = nm
    rbuf[req.a, req.b, :, D:] = gates.astype(BF)

    sent2 = gather_start(req, rbuf, rg_s, rg_r)
    gather_forward(req, rbuf, rg_s, rg_r, sent2)
    c_win.wait()
    c_wdown.wait()
    first = lax.axis_index("req") * EL
    M = RA * T

    def experts(col):
        x = rbuf[:, col, :, :D].reshape(M, D)
        gt = rbuf[:, col, :, D:].reshape(M, LANES).astype(F32)
        gt = gt + pltpu.roll(gt, HD, 1)
        glane = lax.broadcasted_iota(jnp.int32, (M, LANES), 1)

        def up(j, n):
            lo = n * 256
            gate_cols = jnp.dot(x, win[j, :, lo:lo + 256], preferred_element_type=F32)
            up_cols = jnp.dot(x, win[j, :, F + lo:F + lo + 256], preferred_element_type=F32)
            g = jnp.sum(jnp.where(glane == first + j, gt, 0.0), axis=1, keepdims=True)
            act = gate_cols / (1.0 + jnp.exp(-gate_cols)) * up_cols
            hid[j, :, lo:lo + 256] = (act * g).astype(BF)

        @pl.loop(0, EL)
        def _(j):
            for n in range(F // 256):
                up(j, n)

        for n in range(D // 512):
            acc = jnp.zeros((M, 512), F32)
            for j in range(EL):
                acc = acc + jnp.dot(hid[j], wdown[j, :, n * 512:(n + 1) * 512],
                                    preferred_element_type=F32)
            rpart[:, col, :, n * 512:(n + 1) * 512] = acc.astype(BF).reshape(RA, T, 512)

    experts(req.b)
    for e in range(1, RB):
        o = gather_column(req, rbuf, rg_s, rg_r, e)
        experts(o)
        scatter_minor(req, rpart, rrx, rs_s, rs_r, RB - e, sent2)
    mixed = scatter_major(req, rpart, rrx, rs_r, rmid, rrx2, rs2_s, rs2_r, sent2)
    out[...] = (attended + mixed).astype(BF)
    for c in sent + sent2:
        c.wait_send()


def pinned(*arrays):
    return [a if i == 5 else pltpu.with_memory_space_constraint(a, pltpu.HBM)
            for i, a in enumerate(arrays)]


def local(head_n, req_n, residual_in, attn_gain, w_qkv, w_out, kv_cache, lengths,
          moe_gain, w_router, routes, w_in, w_down):
    T = residual_in.shape[0]
    R, kvl, L = kv_cache.shape[:3]
    E = w_router.shape[1]
    EL = w_in.shape[0]
    HB = 2 if head_n % 2 == 0 else 1
    HA = head_n // HB
    RA = 4 if req_n % 4 == 0 else 1
    RB = req_n // RA
    G = R * kvl // 2
    UN, NC = 16, 4
    index = np.arange(HD // 2)
    freq = np.power(THETA, -2.0 * index / HD).astype(np.float32)
    freq = np.tile(freq, 4).reshape(1, LANES)
    vm = pl.BlockSpec(memory_space=pltpu.VMEM)
    sm = pl.BlockSpec(memory_space=pltpu.SMEM)
    hbm = pl.BlockSpec(memory_space=pltpu.HBM)
    dma = pltpu.SemaphoreType.DMA
    V = pltpu.VMEM
    mn = lambda n: max(n, 1)
    layer_out, new_kv = pl.pallas_call(
        functools.partial(body, HA, HB, RA, RB, kvl, UN, NC),
        out_shape=(jax.ShapeDtypeStruct((T, D), BF),
                   jax.ShapeDtypeStruct((R, kvl, LANES), BF)),
        in_specs=[vm, vm, hbm, hbm, hbm, sm, vm, vm, vm, vm, vm, hbm, hbm],
        out_specs=(vm, vm),
        scratch_shapes=[
            V((kvl * (GROUP + 2) * HD, D), BF), V(w_out.shape, BF), V(kv_cache.shape, BF),
            V(w_in.shape, BF), V(w_down.shape, BF),
            V((HA, HB, T, D), BF), V((RA, RB, T, WIDE), BF),
            V((2, G * 8, LANES), F32), V((R, kvl * LANES), F32), V((2, G * 8, LANES), F32),
            V((HA, HB, T, D), BF), V((mn(HB - 1), HA, T, D), BF),
            V((mn(HA - 1), T, D), BF), V((mn(HA - 1), T, D), BF),
            V((RA, RB, T, D), BF), V((mn(RB - 1), RA, T, D), BF),
            V((mn(RA - 1), T, D), BF), V((mn(RA - 1), T, D), BF),
            V((EL, RA * T, F), BF), V((T, LANES), F32), V((T, LANES), F32),
            dma((4,)), dma((NC, 2)),
            dma((HA, HB, CHUNKS)), dma((HA, HB, CHUNKS)), dma((mn(HB - 1), HA, CHUNKS)), dma((mn(HB - 1), HA, CHUNKS)),
            dma((mn(HA - 1), CHUNKS)), dma((mn(HA - 1), CHUNKS)),
            dma((RA, RB, CHUNKS)), dma((RA, RB, CHUNKS)), dma((mn(RB - 1), RA, CHUNKS)), dma((mn(RB - 1), RA, CHUNKS)),
            dma((mn(RA - 1), CHUNKS)), dma((mn(RA - 1), CHUNKS)),
        ],
        compiler_params=pltpu.CompilerParams(
            collective_id=0, has_side_effects=True, vmem_limit_bytes=44 << 20),
        name="layer",
    )(*pinned(residual_in, attn_gain.reshape(D // LANES, LANES),
      w_qkv.transpose(1, 2, 0).reshape(kvl * (GROUP + 2) * HD, D), w_out,
      kv_cache, lengths, lengths.reshape(1, R), freq, moe_gain.reshape(D // LANES, LANES),
      w_router.T, routes.T, w_in, w_down))
    return layer_out, new_kv


def solution(mesh):
    return jax.shard_map(
        functools.partial(local, mesh.shape["head"], mesh.shape["req"]),
        mesh=mesh,
        in_specs=(
            P(("req", "head"), None),
            P(),
            P(None, "head", None),
            P("head", None),
            P("req", "head", None, None),
            P("req"),
            P(),
            P(),
            P(("req", "head"), None),
            P("req", None, None),
            P("req", None, None),
        ),
        out_specs=(P(("req", "head"), None), P("req", "head", None)),
        check_vma=False,
    )
```
